512 devices in a mesh: row: 32 (over z, core), col: 16 (over x, y).
Axes of the slice: x: 4, y: 4, z: 16, core: 2. Of those that a mesh axis runs over, the one named last changes fastest.
Arguments:
- weight: bfloat16 [8192, 53248], P('row', 'col'), may hold values from -6 to 6
- inverse_rows: float32 [512, 53248], P('row', 'col'), as said below
- pruned_index: int32 [512], replicated, may hold values from 0 to 53247, as said below
Outputs:
- pruned_weight: bfloat16 [8192, 53248], P('row', 'col')
- saliency: float32 [8192], P('row')
The draws below stay inside these ranges and needn't reach their ends.
Inputs may be any that keep to these rules, and one draw needn't show every extreme that they name: `pruned_index`: distinct and ascending. Neuron c lies in column shard c // 3328; at most 96 of them lie in one shard, and exactly 96 in one shard. `inverse_rows`: its columns pruned_index form a symmetric positive definite matrix.
All inputs are finite; a program needn't handle non-finite values.
Results may differ from the reference program's by a relative error of at most 0.001.
Values may be sent and summed in bfloat16 or wider, within the bound.
A program may use at most 64 MiB of HBM per device.

```python
import jax
import jax.numpy as jnp
from jax import lax

FF = 53248
PRUNED = 512
ROWS_DEV = 256
ROWS = 8192
COLS_DEV = 3328
CAPACITY = 96
N_ROW = 32


def pruned_draw(key):
    base = jax.random.fold_in(key, 7001)
    key_heavy, key_share, key_pick = jax.random.split(base, 3)
    shards = FF // COLS_DEV
    heavy = jax.random.randint(key_heavy, (), 0, shards)
    shard_ids = jnp.arange(shards)
    shares = jax.random.randint(key_share, (shards,), 2, 6)
    shares = jnp.where(shard_ids == heavy, 0, shares)
    remain = PRUNED - CAPACITY
    counts = shares * remain // jnp.sum(shares)
    leftover = remain - jnp.sum(counts)
    others = jnp.cumsum((shares > 0).astype(jnp.int32)) - 1
    counts = counts + ((others < leftover) & (shares > 0)).astype(jnp.int32)
    counts = jnp.where(shard_ids == heavy, CAPACITY, counts)
    shard_keys = jax.random.split(key_pick, shards)
    orders = jax.vmap(lambda one_key: jax.random.permutation(one_key, COLS_DEV))(shard_keys)
    chosen = orders < counts[:, None]
    return jnp.nonzero(chosen.reshape(-1), size=PRUNED)[0].astype(jnp.int32)


def draw_pruned_index(key, part):
    return pruned_draw(key)


def draw_inverse_rows(key, part):
    index = pruned_draw(key)
    key_gauss = jax.random.fold_in(jax.random.fold_in(key, 7002), 0)
    key_rest = jax.random.fold_in(jax.random.fold_in(key, 7002), 1)
    key_spread = jax.random.fold_in(jax.random.fold_in(key, 7002), 3)
    gauss = jax.random.normal(key_gauss, (PRUNED, PRUNED), jnp.float32)
    spread = jnp.exp(jax.random.uniform(key_spread, (PRUNED,), jnp.float32, -3.0, 3.0))
    block = jnp.dot(gauss * spread[None, :], gauss.T, precision=lax.Precision.HIGHEST) / PRUNED
    block = block + 0.05 * jnp.eye(PRUNED, dtype=jnp.float32)
    block = 0.5 * (block + block.T)
    others = jax.random.normal(key_rest, (PRUNED, FF), jnp.float32) * PRUNED ** (-0.5)
    full = others.at[:, index].set(block)
    return full.astype(jnp.float32)


def steps_of(own_key, shape, cuts, least, largest):
    level, own = 1.0, jax.random.fold_in(own_key, 6)
    for axis_at, parts in cuts:
        heights = jnp.exp(jax.random.uniform(jax.random.fold_in(own, axis_at), (parts,), jnp.float32, least / len(cuts), largest / len(cuts)))
        level = level * jnp.repeat(heights, shape[axis_at] // parts).reshape([-1 if axis == axis_at else 1 for axis in range(len(shape))])
    return level


def bell_draw(own_key, shape, deviation, reach, cuts=(), kind=jnp.bfloat16):
    level = steps_of(own_key, shape, cuts, -0.22, 0.18) if cuts else 1.0
    result = jax.random.normal(own_key, shape, jnp.float32) * deviation * level
    return jnp.minimum(jnp.maximum(result, -reach), reach).astype(kind)


def setup_inputs(seed: int = 0) -> dict:
    key_of = jax.random.split(jax.random.key(seed), 4)
    weight = bell_draw(key_of[0], (ROWS, FF), 1.0, 6.0, ((0, 32), (1, 16)))
    inverse_rows = draw_inverse_rows(jax.random.fold_in(key_of[3], 71), 0)
    pruned_index = draw_pruned_index(jax.random.fold_in(key_of[3], 71), 0)
    return {"weight": weight, "inverse_rows": inverse_rows, "pruned_index": pruned_index}


def reference(weight, inverse_rows, pruned_index):
    weight_pruned = jnp.take(weight, pruned_index, axis=1).astype(jnp.float32)
    schur_block = jnp.take(inverse_rows, pruned_index, axis=1)
    factor_low = jnp.linalg.cholesky(schur_block)
    solved = jax.scipy.linalg.cho_solve((factor_low, True), weight_pruned.T).T

    def one_block(pair):
        weight_block, solved_block = pair
        correction = jnp.dot(solved_block.astype(jnp.float32), inverse_rows.astype(jnp.float32), precision=lax.Precision.HIGHEST, preferred_element_type=jnp.float32)
        return (weight_block.astype(jnp.float32) - correction).astype(jnp.bfloat16)
    updated = lax.map(one_block, (weight.reshape(N_ROW, ROWS_DEV, FF), solved.reshape(N_ROW, ROWS_DEV, PRUNED)))
    saliency = jnp.sum(solved * weight_pruned, axis=1) / (2.0 * PRUNED)
    return (updated.reshape(ROWS, FF), saliency)
```

```python
import functools

import jax
import jax.numpy as jnp
from jax import lax
from jax.experimental import pallas as pl
from jax.experimental.pallas import tpu as pltpu
from jax.sharding import PartitionSpec as P

F32, BF16 = jnp.float32, jnp.bfloat16
LANES = 128


def split3(x):
    hi = x.astype(BF16)
    r = x - hi.astype(F32)
    mid = r.astype(BF16)
    lo = (r - mid.astype(F32)).astype(BF16)
    return hi, mid, lo

def bsub(x, k):
    return jnp.broadcast_to(x[k:k+1, :], x.shape)

def inv8(cols):
    sub = lax.broadcasted_iota(jnp.int32, (8, 128), 0)
    for k in range(8):
        t = [bsub(c, k) for c in cols]
        r = 1.0 / t[k]
        ck = cols[k]
        new = []
        for j in range(8):
            if j == k:
                new.append(jnp.where(sub == k, r, -(ck * r)))
            else:
                new.append(jnp.where(sub == k, t[j] * r, cols[j] - (ck * t[j]) * r))
        cols = new
    return cols

def panel_gj(P, kb, nb, nt):
    lane = lax.broadcasted_iota(jnp.int32, (8, 128), 1)
    sub = lax.broadcasted_iota(jnp.int32, (8, 128), 0)
    for g in range(nb):
        col0 = kb + g * 8
        pt, l0 = col0 // 128, col0 % 128
        C = [[jnp.broadcast_to(P[i][pt][:, l0 + j:l0 + j + 1], (8, 128)) for j in range(8)] for i in range(nb)]
        Dinv = inv8(C[g])
        inside = (lane >= l0) & (lane < l0 + 8)
        eye = jnp.where(lane - l0 == sub, 1.0, 0.0)
        for i in range(nb):
            P[i][pt] = jnp.where(inside, eye if i == g else 0.0, P[i][pt])
        U = []
        for t in range(nt):
            acc = Dinv[0] * bsub(P[g][t], 0)
            for j in range(1, 8):
                acc = acc + Dinv[j] * bsub(P[g][t], j)
            U.append(acc)
        for t in range(nt):
            ub = [bsub(U[t], j) for j in range(8)]
            for i in range(nb):
                if i != g:
                    acc = P[i][t]
                    for j in range(8):
                        acc = acc - C[i][j] * ub[j]
                    P[i][t] = acc
            P[g][t] = U[t]
    return P

def solve_kernel(s_ref, w_ref, hi_ref, lo_ref, sal_ref, m, *, B=32, n=512):
    nw = w_ref.shape[0]
    nb, nt = B // 8, n // 128
    m[0:n, :] = s_ref[...]
    m[n:n + nw, :] = w_ref[...].astype(F32)
    rows = n + nw
    lane = lax.broadcasted_iota(jnp.int32, (8, 128), 1)
    sub = lax.broadcasted_iota(jnp.int32, (8, 128), 0)
    def load_panel(k):
        return [[m[k*B+g*8:k*B+g*8+8, t*128:t*128+128] for t in range(nt)] for g in range(nb)]
    P = load_panel(0)
    for k in range(n // B):
        kb = k * B
        P = panel_gj(P, kb, nb, nt)
        pt, l0 = kb // 128, kb % 128
        for g in range(nb):
            x = P[g][pt]
            inside = (lane >= l0) & (lane < l0 + B)
            eye = jnp.where(lane - l0 == sub + g * 8, 1.0, 0.0)
            P[g][pt] = jnp.where(inside, eye - x, x)
        U = jnp.concatenate([jnp.concatenate(P[g], axis=1) for g in range(nb)], axis=0)
        uh, um, ul = split3(U)
        us = jnp.concatenate([uh, um, uh, ul, um, uh], axis=0)
        def upd(r0, r1):
            C = m[r0:r1, pt*128:pt*128+128][:, l0:l0 + B]
            ch, cm, cl = split3(C)
            cs = jnp.concatenate([ch, ch, cm, ch, cm, cl], axis=1)
            return m[r0:r1, :] - jnp.dot(cs, us, preferred_element_type=F32)
        nr0 = (k + 1) * B
        if k + 1 < n // B:
            new = upd(nr0, nr0 + B)
            P = [[new[g*8:g*8+8, t*128:t*128+128] for t in range(nt)] for g in range(nb)]
            nr0 += B
        m[nr0:rows, :] = upd(nr0, rows)
    X = m[n:rows, :]
    h = X.astype(BF16)
    hi_ref[...] = h
    lo_ref[...] = (X - h.astype(F32)).astype(BF16)
    sal_ref[...] = jnp.sum(X * w_ref[...].astype(F32), axis=1, keepdims=True) / (2.0 * n)

def solve(S, W, B=32):
    n, nw = S.shape[0], W.shape[0]
    return pl.pallas_call(
        functools.partial(solve_kernel, B=B, n=n),
        out_shape=(jax.ShapeDtypeStruct((nw, n), BF16), jax.ShapeDtypeStruct((nw, n), BF16), jax.ShapeDtypeStruct((nw, 1), F32)),
        in_specs=[pl.BlockSpec(memory_space=pltpu.VMEM)] * 2,
        out_specs=tuple(pl.BlockSpec(memory_space=pltpu.VMEM) for _ in range(3)),
        scratch_shapes=[pltpu.VMEM((n + nw, n), F32)],
        name="solve",
    )(S, W)

MESH_ID = pl.DeviceIdType.MESH


def exchange_kernel(idx_ref, w_ref, inv_ref, s_out, wsel_out, sbuf, wbuf, place, sblk,
                    xs_send, xs_recv, xw_send, xw_recv, up_send, up_recv, dn_send, dn_recv, pr_send, pr_recv):
    n_row, n_col = lax.axis_size("row"), lax.axis_size("col")
    n_z = n_row // 2
    rows, width = w_ref.shape
    n = idx_ref.shape[1]
    row, col = lax.axis_index("row"), lax.axis_index("col")
    z, core = row // 2, lax.rem(row, 2)
    up = lax.rem(row + 2, n_row)
    down = lax.rem(row + n_row - 2, n_row)
    partner = row + 1 - 2 * core

    barrier = pltpu.get_barrier_semaphore()
    for k in range(1, n_col):
        pl.semaphore_signal(barrier, inc=1, device_id={"row": row, "col": lax.rem(col + k, n_col)}, device_id_type=MESH_ID)
    for other in (up, down, partner):
        pl.semaphore_signal(barrier, inc=1, device_id={"row": other, "col": col}, device_id_type=MESH_ID)

    idx = idx_ref[...]
    anchor = col * width
    start = jnp.sum(jnp.where(idx < anchor, 1.0, 0.0), axis=1, keepdims=True)
    own = jnp.where((idx >= anchor) & (idx < anchor + width), 1.0, 0.0)
    high = idx // 256
    low = idx - high * 256
    sub8 = lax.broadcasted_iota(jnp.int32, (8, n), 0)
    facts = jnp.where(sub8 == 0, high.astype(F32), jnp.where(sub8 == 1, low.astype(F32), jnp.where(sub8 == 2, own, 0.0)))
    at = lax.broadcasted_iota(jnp.int32, (n, LANES), 0).astype(F32)
    slot = lax.broadcasted_iota(jnp.int32, (n, LANES), 1).astype(F32)
    window = jnp.where(at == slot + start, 1.0, 0.0).astype(BF16)
    picked = jnp.dot(facts.astype(BF16), window, preferred_element_type=F32)
    local = jnp.where(picked[2:3, :] > 0.5, picked[0:1, :] * 256.0 + picked[1:2, :] - anchor.astype(F32), -1.0)
    column = lax.broadcasted_iota(jnp.int32, (width, LANES), 0).astype(F32)
    picker = jnp.where(column == local, 1.0, 0.0).astype(BF16)

    ih, im, il = split3(inv_ref[...])
    part = inv_ref.shape[0]
    three = jnp.dot(jnp.concatenate([ih, im, il], axis=0), picker, preferred_element_type=F32)
    sbuf[col] = three[0:part] + three[part:2 * part] + three[2 * part:3 * part]
    wbuf[col] = jnp.dot(w_ref[...], picker, preferred_element_type=F32).astype(BF16)

    pl.semaphore_wait(barrier, n_col + 2)
    s_copies, w_copies = [], []
    for k in range(1, n_col):
        target = {"row": row, "col": lax.rem(col + k, n_col)}
        c = pltpu.make_async_remote_copy(sbuf.at[col], sbuf.at[col], xs_send.at[k], xs_recv.at[k], device_id=target, device_id_type=MESH_ID)
        c.start()
        s_copies.append(c)
    for k in range(1, n_col):
        target = {"row": row, "col": lax.rem(col + k, n_col)}
        c = pltpu.make_async_remote_copy(wbuf.at[col], wbuf.at[col], xw_send.at[k], xw_recv.at[k], device_id=target, device_id_type=MESH_ID)
        c.start()
        w_copies.append(c)

    shard = lax.broadcasted_iota(jnp.int32, (n_col, n), 0)
    starts = jnp.sum(jnp.where(idx < shard * width, 1.0, 0.0), axis=1, keepdims=True)
    mine = (idx >= shard * width) & (idx < (shard + 1) * width)
    base = jnp.sum(jnp.where(mine, (shard * LANES).astype(F32) - starts, 0.0), axis=0, keepdims=True)
    slot_of = base + lax.broadcasted_iota(jnp.int32, (1, n), 1).astype(F32)
    for c in range(n_col):
        q = lax.broadcasted_iota(jnp.int32, (LANES, n), 0).astype(F32) + float(c * LANES)
        place[c * LANES:(c + 1) * LANES, :] = jnp.where(q == slot_of, 1.0, 0.0).astype(BF16)

    for c in s_copies:
        c.wait()
    joined = jnp.concatenate([sbuf[c] for c in range(n_col)], axis=1)
    jh, jm, jl = split3(joined)
    three = jnp.dot(jnp.concatenate([jh, jm, jl], axis=0), place[...], preferred_element_type=F32)
    sblk[z, core] = three[0:part] + three[part:2 * part] + three[2 * part:3 * part]

    def send(block, owner_core, target_row, send_sem, recv_sem):
        c = pltpu.make_async_remote_copy(sblk.at[block, owner_core], sblk.at[block, owner_core], send_sem, recv_sem,
                                         device_id={"row": target_row, "col": col}, device_id_type=MESH_ID)
        c.start()
        return c
    ups, downs = n_z // 2, n_z - 1 - n_z // 2
    held = [send(z, core, partner, pr_send.at[0], pr_recv.at[0])]
    flying_up = send(z, core, up, up_send.at[0], up_recv.at[0])
    flying_dn = send(z, core, down, dn_send.at[0], dn_recv.at[0])
    for s in range(1, ups + 1):
        block = lax.rem(z + n_z - s, n_z)
        flying_up.wait()
        if s < ups:
            flying_up = send(block, core, up, up_send.at[s], up_recv.at[s])
        held.append(send(block, core, partner, pr_send.at[s], pr_recv.at[s]))
        if s <= downs:
            block = lax.rem(z + s, n_z)
            flying_dn.wait()
            if s < downs:
                flying_dn = send(block, core, down, dn_send.at[s], dn_recv.at[s])
            held.append(send(block, core, partner, pr_send.at[ups + s], pr_recv.at[ups + s]))
    for c in w_copies:
        c.wait()
    wj = jnp.concatenate([wbuf[c] for c in range(n_col)], axis=1)
    wsel_out[...] = jnp.dot(wj, place[...], preferred_element_type=F32).astype(BF16)
    for c in held:
        c.wait()
    for b in range(n_z):
        for c in range(2):
            r0 = (b * 2 + c) * part
            s_out[r0:r0 + part, :] = sblk[b, c]


def exchange(idx, weight, inverse_rows, n_row, n_col):
    n = idx.shape[1]
    rows, part = weight.shape[0], inverse_rows.shape[0]
    n_z = n_row // 2
    dma = pltpu.SemaphoreType.DMA
    vm = pl.BlockSpec(memory_space=pltpu.VMEM)
    return pl.pallas_call(
        exchange_kernel,
        out_shape=(jax.ShapeDtypeStruct((n, n), F32), jax.ShapeDtypeStruct((rows, n), BF16)),
        in_specs=[vm] * 3,
        out_specs=(vm, vm),
        scratch_shapes=[
            pltpu.VMEM((n_col, part, LANES), F32),
            pltpu.VMEM((n_col, rows, LANES), BF16),
            pltpu.VMEM((n_col * LANES, n), BF16),
            pltpu.VMEM((n_z, 2, part, n), F32),
            dma((n_col,)), dma((n_col,)), dma((n_col,)), dma((n_col,)),
            dma((n_z,)), dma((n_z,)), dma((n_z,)), dma((n_z,)), dma((n_z,)), dma((n_z,)),
        ],
        compiler_params=pltpu.CompilerParams(collective_id=0, has_side_effects=True),
        name="exchange",
    )(idx, weight, inverse_rows)


def update_kernel(w_ref, inv_ref, hi_ref, lo_ref, out_ref):
    inv = inv_ref[...]
    ih = inv.astype(BF16)
    il = (inv - ih.astype(F32)).astype(BF16)
    hi, lo = hi_ref[...], lo_ref[...]
    left = jnp.concatenate([hi, lo, hi], axis=1)
    right = jnp.concatenate([ih, ih, il], axis=0)
    out_ref[...] = (w_ref[...].astype(F32) - jnp.dot(left, right, preferred_element_type=F32)).astype(BF16)


def update(weight, inverse_all, hi, lo, tile=256):
    rows, width = weight.shape
    n = hi.shape[1]
    return pl.pallas_call(
        update_kernel,
        grid=(width // tile,),
        out_shape=jax.ShapeDtypeStruct((rows, width), BF16),
        in_specs=[pl.BlockSpec((rows, tile), lambda i: (0, i)), pl.BlockSpec((n, tile), lambda i: (0, i)),
                  pl.BlockSpec((rows, n), lambda i: (0, 0)), pl.BlockSpec((rows, n), lambda i: (0, 0))],
        out_specs=pl.BlockSpec((rows, tile), lambda i: (0, i)),
        name="update",
    )(weight, inverse_all, hi, lo)


def solution(mesh):
    n_row, n_col = mesh.shape["row"], mesh.shape["col"]

    def body(weight, inverse_rows, pruned_index):
        inverse_all = lax.all_gather(inverse_rows, "row", axis=0, tiled=True)
        schur, chosen = exchange(pruned_index[None, :], weight, inverse_rows, n_row, n_col)
        hi, lo, sal = solve(schur, chosen)
        return update(weight, inverse_all, hi, lo), sal[:, 0]

    return jax.shard_map(
        body,
        mesh=mesh,
        in_specs=(P("row", "col"), P("row", "col"), P()),
        out_specs=(P("row", "col"), P("row")),
        check_vma=False,
    )
```

```python
import functools

import jax
import jax.numpy as jnp
from jax import lax
from jax.experimental import pallas as pl
from jax.experimental.pallas import tpu as pltpu
from jax.sharding import PartitionSpec as P

F32, BF16 = jnp.float32, jnp.bfloat16
LANES = 128
BLOCK = 32


def split3(x):
    hi = x.astype(BF16)
    r = x - hi.astype(F32)
    mid = r.astype(BF16)
    lo = (r - mid.astype(F32)).astype(BF16)
    return hi, mid, lo

def bsub(x, k):
    return jnp.broadcast_to(x[k:k+1, :], x.shape)

def inv8(cols):
    sub = lax.broadcasted_iota(jnp.int32, (8, 128), 0)
    for k in range(8):
        t = [bsub(c, k) for c in cols]
        r = 1.0 / t[k]
        ck = cols[k]
        new = []
        for j in range(8):
            if j == k:
                new.append(jnp.where(sub == k, r, -(ck * r)))
            else:
                new.append(jnp.where(sub == k, t[j] * r, cols[j] - (ck * t[j]) * r))
        cols = new
    return cols

def panel_gj(P, kb, nb, nt):
    lane = lax.broadcasted_iota(jnp.int32, (8, 128), 1)
    sub = lax.broadcasted_iota(jnp.int32, (8, 128), 0)
    for g in range(nb):
        col0 = kb + g * 8
        pt, l0 = col0 // 128, col0 % 128
        C = [[jnp.broadcast_to(P[i][pt][:, l0 + j:l0 + j + 1], (8, 128)) for j in range(8)] for i in range(nb)]
        Dinv = inv8(C[g])
        inside = (lane >= l0) & (lane < l0 + 8)
        eye = jnp.where(lane - l0 == sub, 1.0, 0.0)
        for i in range(nb):
            P[i][pt] = jnp.where(inside, eye if i == g else 0.0, P[i][pt])
        U = []
        for t in range(nt):
            acc = Dinv[0] * bsub(P[g][t], 0)
            for j in range(1, 8):
                acc = acc + Dinv[j] * bsub(P[g][t], j)
            U.append(acc)
        for t in range(nt):
            ub = [bsub(U[t], j) for j in range(8)]
            for i in range(nb):
                if i != g:
                    acc = P[i][t]
                    for j in range(8):
                        acc = acc - C[i][j] * ub[j]
                    P[i][t] = acc
            P[g][t] = U[t]
    return P


def eliminate(m, n, after):
    rows = m.shape[0]
    nb, nt = BLOCK // 8, n // 128
    lane = lax.broadcasted_iota(jnp.int32, (8, 128), 1)
    sub = lax.broadcasted_iota(jnp.int32, (8, 128), 0)
    P = [[m[g*8:g*8+8, t*128:t*128+128] for t in range(nt)] for g in range(nb)]
    for k in range(n // BLOCK):
        kb = k * BLOCK
        P = panel_gj(P, kb, nb, nt)
        pt, l0 = kb // 128, kb % 128
        for g in range(nb):
            x = P[g][pt]
            inside = (lane >= l0) & (lane < l0 + BLOCK)
            eye = jnp.where(lane - l0 == sub + g * 8, 1.0, 0.0)
            P[g][pt] = jnp.where(inside, eye - x, x)
        U = jnp.concatenate([jnp.concatenate(P[g], axis=1) for g in range(nb)], axis=0)
        uh, um, ul = split3(U)
        us = jnp.concatenate([uh, um, uh, ul, um, uh], axis=0)

        def upd(r0, r1):
            C = m[r0:r1, pt*128:pt*128+128][:, l0:l0 + BLOCK]
            ch, cm, cl = split3(C)
            cs = jnp.concatenate([ch, ch, cm, ch, cm, cl], axis=1)
            return m[r0:r1, :] - jnp.dot(cs, us, preferred_element_type=F32)
        nr0 = (k + 1) * BLOCK
        if k + 1 < n // BLOCK:
            new = upd(nr0, nr0 + BLOCK)
            P = [[new[g*8:g*8+8, t*128:t*128+128] for t in range(nt)] for g in range(nb)]
            nr0 += BLOCK
        m[nr0:rows, :] = upd(nr0, rows)
        after(k)

MESH_ID = pl.DeviceIdType.MESH


def step_kernel(idx_ref, w_ref, inv_ref, out_ref, sal_ref, sbuf, wbuf, place, sblk, m, gat, outv,
                xs_send, xs_recv, xw_send, xw_recv, up_send, up_recv, dn_send, dn_recv, pr_send, pr_recv,
                gu_send, gu_recv, gd_send, gd_recv, gp_send, gp_recv, out_sem):
    n_row, n_col = lax.axis_size("row"), lax.axis_size("col")
    n_z = n_row // 2
    rows, width = w_ref.shape
    n = idx_ref.shape[1]
    row, col = lax.axis_index("row"), lax.axis_index("col")
    z, core = row // 2, lax.rem(row, 2)
    up = lax.rem(row + 2, n_row)
    down = lax.rem(row + n_row - 2, n_row)
    partner = row + 1 - 2 * core

    barrier = pltpu.get_barrier_semaphore()
    for k in range(1, n_col):
        pl.semaphore_signal(barrier, inc=1, device_id={"row": row, "col": lax.rem(col + k, n_col)}, device_id_type=MESH_ID)
    for other in (up, down, partner):
        pl.semaphore_signal(barrier, inc=1, device_id={"row": other, "col": col}, device_id_type=MESH_ID)

    idx = idx_ref[...]
    anchor = col * width
    start = jnp.sum(jnp.where(idx < anchor, 1.0, 0.0), axis=1, keepdims=True)
    own = jnp.where((idx >= anchor) & (idx < anchor + width), 1.0, 0.0)
    high = idx // 256
    low = idx - high * 256
    sub8 = lax.broadcasted_iota(jnp.int32, (8, n), 0)
    facts = jnp.where(sub8 == 0, high.astype(F32), jnp.where(sub8 == 1, low.astype(F32), jnp.where(sub8 == 2, own, 0.0)))
    at = lax.broadcasted_iota(jnp.int32, (n, LANES), 0).astype(F32)
    slot = lax.broadcasted_iota(jnp.int32, (n, LANES), 1).astype(F32)
    window = jnp.where(at == slot + start, 1.0, 0.0).astype(BF16)
    picked = jnp.dot(facts.astype(BF16), window, preferred_element_type=F32)
    local = jnp.where(picked[2:3, :] > 0.5, picked[0:1, :] * 256.0 + picked[1:2, :] - anchor.astype(F32), -1.0)
    column = lax.broadcasted_iota(jnp.int32, (width, LANES), 0).astype(F32)
    picker = jnp.where(column == local, 1.0, 0.0).astype(BF16)

    ih, im, il = split3(inv_ref[...])
    part = inv_ref.shape[0]
    gat[0, z, core] = ih
    gat[1, z, core] = im
    three = jnp.dot(jnp.concatenate([ih, im, il], axis=0), picker, preferred_element_type=F32)
    sbuf[col] = three[0:part] + three[part:2 * part] + three[2 * part:3 * part]
    wbuf[col] = jnp.dot(w_ref[...], picker, preferred_element_type=F32).astype(BF16)

    pl.semaphore_wait(barrier, n_col + 2)
    ups, downs = n_z // 2, n_z - 1 - n_z // 2
    sent = []

    def push(p, block, target_row, send_sem, recv_sem):
        c = pltpu.make_async_remote_copy(gat.at[p, block, core], gat.at[p, block, core], send_sem, recv_sem,
                                         device_id={"row": target_row, "col": col}, device_id_type=MESH_ID)
        c.start()
        return c
    s_copies, w_copies = [], []
    for k in range(1, n_col):
        target = {"row": row, "col": lax.rem(col + k, n_col)}
        c = pltpu.make_async_remote_copy(sbuf.at[col], sbuf.at[col], xs_send.at[k], xs_recv.at[k], device_id=target, device_id_type=MESH_ID)
        c.start()
        s_copies.append(c)
    for k in range(1, n_col):
        target = {"row": row, "col": lax.rem(col + k, n_col)}
        c = pltpu.make_async_remote_copy(wbuf.at[col], wbuf.at[col], xw_send.at[k], xw_recv.at[k], device_id=target, device_id_type=MESH_ID)
        c.start()
        w_copies.append(c)

    fly_up, fly_dn, mates = {}, {}, []
    for p in range(2):
        fly_up[p] = push(p, z, up, gu_send.at[p, 0], gu_recv.at[p, 0])
        fly_dn[p] = push(p, z, down, gd_send.at[p, 0], gd_recv.at[p, 0])
        mates.append(push(p, z, partner, gp_send.at[p, 0], gp_recv.at[p, 0]))

    def service(piece):
        s, p = piece // 2 + 1, piece % 2
        block = lax.rem(z + n_z - s, n_z)
        fly_up[p].wait()
        if s < ups:
            fly_up[p] = push(p, block, up, gu_send.at[p, s], gu_recv.at[p, s])
        mates.append(push(p, block, partner, gp_send.at[p, s], gp_recv.at[p, s]))
        if s <= downs:
            block = lax.rem(z + s, n_z)
            fly_dn[p].wait()
            if s < downs:
                fly_dn[p] = push(p, block, down, gd_send.at[p, s], gd_recv.at[p, s])
            mates.append(push(p, block, partner, gp_send.at[p, ups + s], gp_recv.at[p, ups + s]))

    shard = lax.broadcasted_iota(jnp.int32, (n_col, n), 0)
    starts = jnp.sum(jnp.where(idx < shard * width, 1.0, 0.0), axis=1, keepdims=True)
    mine = (idx >= shard * width) & (idx < (shard + 1) * width)
    base = jnp.sum(jnp.where(mine, (shard * LANES).astype(F32) - starts, 0.0), axis=0, keepdims=True)
    slot_of = base + lax.broadcasted_iota(jnp.int32, (1, n), 1).astype(F32)
    for c in range(n_col):
        q = lax.broadcasted_iota(jnp.int32, (LANES, n), 0).astype(F32) + float(c * LANES)
        place[c * LANES:(c + 1) * LANES, :] = jnp.where(q == slot_of, 1.0, 0.0).astype(BF16)

    for c in s_copies:
        c.wait()
    joined = jnp.concatenate([sbuf[c] for c in range(n_col)], axis=1)
    jh, jm, jl = split3(joined)
    three = jnp.dot(jnp.concatenate([jh, jm, jl], axis=0), place[...], preferred_element_type=F32)
    sblk[z, core] = three[0:part] + three[part:2 * part] + three[2 * part:3 * part]

    def send(block, owner_core, target_row, send_sem, recv_sem):
        c = pltpu.make_async_remote_copy(sblk.at[block, owner_core], sblk.at[block, owner_core], send_sem, recv_sem,
                                         device_id={"row": target_row, "col": col}, device_id_type=MESH_ID)
        c.start()
        return c
    held = [send(z, core, partner, pr_send.at[0], pr_recv.at[0])]
    flying_up = send(z, core, up, up_send.at[0], up_recv.at[0])
    flying_dn = send(z, core, down, dn_send.at[0], dn_recv.at[0])
    for s in range(1, ups + 1):
        block = lax.rem(z + n_z - s, n_z)
        flying_up.wait()
        if s < ups:
            flying_up = send(block, core, up, up_send.at[s], up_recv.at[s])
        held.append(send(block, core, partner, pr_send.at[s], pr_recv.at[s]))
        if s <= downs:
            block = lax.rem(z + s, n_z)
            flying_dn.wait()
            if s < downs:
                flying_dn = send(block, core, down, dn_send.at[s], dn_recv.at[s])
            held.append(send(block, core, partner, pr_send.at[ups + s], pr_recv.at[ups + s]))
        if s > 1:
            service(s - 2)
    for c in w_copies:
        c.wait()
    wj = jnp.concatenate([wbuf[c] for c in range(n_col)], axis=1)
    chosen = jnp.dot(wj, place[...], preferred_element_type=F32)
    m[n:n + rows, :] = chosen
    for c in held:
        c.wait()
    for b in range(n_z):
        for c in range(2):
            r0 = (b * 2 + c) * part
            m[r0:r0 + part, :] = sblk[b, c]
    total = 2 * ups
    done = [ups - 1]

    def after(k):
        goal = ups - 1 + ((k + 1) * (total - ups + 1)) // (n // BLOCK)
        while done[0] < goal:
            service(done[0])
            done[0] += 1

    eliminate(m, n, after)
    solved = m[n:n + rows, :]
    hi = solved.astype(BF16)
    lo = (solved - hi.astype(F32)).astype(BF16)
    prod = solved * jnp.dot(wj, place[...], preferred_element_type=F32)
    folded = prod[:, 0:128]
    for t in range(1, n // 128):
        folded = folded + prod[:, t * 128:(t + 1) * 128]
    sal_ref[...] = jnp.sum(folded.T, axis=0, keepdims=True) / (2.0 * n)
    for c in mates:
        c.wait()
    both = jnp.concatenate([hi, lo], axis=0)
    units = width // 256
    cuts = [256 * (units * t // 4) for t in range(5)]
    stores = []
    for t in range(4):
        cs, tile = slice(cuts[t], cuts[t + 1]), cuts[t + 1] - cuts[t]
        gh = gat[0, :, :, :, cs].reshape(n, tile)
        gl = gat[1, :, :, :, cs].reshape(n, tile)
        a = jnp.dot(both, gh, preferred_element_type=F32)
        acc = a[0:rows] + a[rows:2 * rows] + jnp.dot(hi, gl, preferred_element_type=F32)
        outv[:, cs] = (w_ref[:, cs].astype(F32) - acc).astype(BF16)
        c = pltpu.make_async_copy(outv.at[:, cs], out_ref.at[:, cs], out_sem.at[t])
        c.start()
        stores.append(c)
    for c in stores:
        c.wait()


def step(idx, weight, inverse_rows, n_row, n_col):
    n = idx.shape[1]
    rows, width = weight.shape
    part = inverse_rows.shape[0]
    n_z = n_row // 2
    dma = pltpu.SemaphoreType.DMA
    vm = pl.BlockSpec(memory_space=pltpu.VMEM)
    return pl.pallas_call(
        step_kernel,
        out_shape=(jax.ShapeDtypeStruct((rows, width), BF16), jax.ShapeDtypeStruct((1, rows), F32)),
        in_specs=[vm] * 3,
        out_specs=(pl.BlockSpec(memory_space=pl.ANY), vm),
        scratch_shapes=[
            pltpu.VMEM((n_col, part, LANES), F32),
            pltpu.VMEM((n_col, rows, LANES), BF16),
            pltpu.VMEM((n_col * LANES, n), BF16),
            pltpu.VMEM((n_z, 2, part, n), F32),
            pltpu.VMEM((n + rows, n), F32),
            pltpu.VMEM((2, n_z, 2, part, width), BF16),
            pltpu.VMEM((rows, width), BF16),
            dma((n_col,)), dma((n_col,)), dma((n_col,)), dma((n_col,)),
            dma((n_z,)), dma((n_z,)), dma((n_z,)), dma((n_z,)), dma((n_z,)), dma((n_z,)),
            dma((2, n_z)), dma((2, n_z)), dma((2, n_z)), dma((2, n_z)), dma((2, n_z)), dma((2, n_z)),
            dma((4,)),
        ],
        compiler_params=pltpu.CompilerParams(collective_id=0, has_side_effects=True, vmem_limit_bytes=60 << 20),
        name="step",
    )(idx, weight, inverse_rows)


def solution(mesh):
    n_row, n_col = mesh.shape["row"], mesh.shape["col"]

    def body(weight, inverse_rows, pruned_index):
        out, sal = step(pruned_index[None, :], weight, inverse_rows, n_row, n_col)
        return out, sal[0]

    return jax.shard_map(
        body,
        mesh=mesh,
        in_specs=(P("row", "col"), P("row", "col"), P()),
        out_specs=(P("row", "col"), P("row")),
        check_vma=False,
    )
```

```python
import functools

import jax
import jax.numpy as jnp
from jax import lax
from jax.experimental import pallas as pl
from jax.experimental.pallas import tpu as pltpu
from jax.sharding import PartitionSpec as P

F32, BF16 = jnp.float32, jnp.bfloat16
LANES = 128
BLOCK = 32
PACE = (0, 1, 1, 1, 1, 1, 1, 1, 1)
MID = (0, 1, 0, 1, 0, 1, 0, 1, 1)


def split3(x):
    hi = x.astype(BF16)
    r = x - hi.astype(F32)
    mid = r.astype(BF16)
    lo = (r - mid.astype(F32)).astype(BF16)
    return hi, mid, lo

def bsub(x, k):
    return jnp.broadcast_to(x[k:k+1, :], x.shape)

def inv8(cols):
    sub = lax.broadcasted_iota(jnp.int32, (8, 128), 0)
    for k in range(8):
        t = [bsub(c, k) for c in cols]
        r = 1.0 / t[k]
        ck = cols[k]
        new = []
        for j in range(8):
            if j == k:
                new.append(jnp.where(sub == k, r, -(ck * r)))
            else:
                new.append(jnp.where(sub == k, t[j] * r, cols[j] - (ck * t[j]) * r))
        cols = new
    return cols

def panel_gj(P, kb, nb, nt):
    lane = lax.broadcasted_iota(jnp.int32, (8, 128), 1)
    sub = lax.broadcasted_iota(jnp.int32, (8, 128), 0)
    for g in range(nb):
        col0 = kb + g * 8
        pt, l0 = col0 // 128, col0 % 128
        C = [[jnp.broadcast_to(P[i][pt][:, l0 + j:l0 + j + 1], (8, 128)) for j in range(8)] for i in range(nb)]
        Dinv = inv8(C[g])
        inside = (lane >= l0) & (lane < l0 + 8)
        eye = jnp.where(lane - l0 == sub, 1.0, 0.0)
        for i in range(nb):
            P[i][pt] = jnp.where(inside, eye if i == g else 0.0, P[i][pt])
        U = []
        for t in range(nt):
            acc = Dinv[0] * bsub(P[g][t], 0)
            for j in range(1, 8):
                acc = acc + Dinv[j] * bsub(P[g][t], j)
            U.append(acc)
        for t in range(nt):
            ub = [bsub(U[t], j) for j in range(8)]
            for i in range(nb):
                if i != g:
                    acc = P[i][t]
                    for j in range(8):
                        acc = acc - C[i][j] * ub[j]
                    P[i][t] = acc
            P[g][t] = U[t]
    return P


def stack_left(x):
    h, m, l = split3(x)
    return jnp.concatenate([h, h, m, h, m, l], axis=1)


def pivot(rows, kb):
    n = rows.shape[1]
    nb, nt = BLOCK // 8, n // LANES
    lane = lax.broadcasted_iota(jnp.int32, (8, LANES), 1)
    sub = lax.broadcasted_iota(jnp.int32, (8, LANES), 0)
    P = [[rows[g * 8:g * 8 + 8, t * LANES:(t + 1) * LANES] for t in range(nt)] for g in range(nb)]
    P = panel_gj(P, kb, nb, nt)
    pt, l0 = kb // LANES, kb % LANES
    inside = (lane >= l0) & (lane < l0 + BLOCK)
    upd, new = [], []
    for g in range(nb):
        eye = jnp.where(lane - l0 == sub + g * 8, 1.0, 0.0)
        urow = [jnp.where(inside, eye - x, x) if t == pt else x for t, x in enumerate(P[g])]
        nrow = [jnp.where(inside, x, -x) if t == pt else -x for t, x in enumerate(P[g])]
        upd.append(jnp.concatenate(urow, axis=1))
        new.append(jnp.concatenate(nrow, axis=1))
    uh, um, ul = split3(jnp.concatenate(upd, axis=0))
    return jnp.concatenate([uh, um, uh, ul, um, uh], axis=0), jnp.concatenate(new, axis=0)


def reduced(x, kb, right):
    return x - jnp.dot(stack_left(x[:, kb:kb + BLOCK]), right, preferred_element_type=F32)


MESH_ID = pl.DeviceIdType.MESH


def step_kernel(idx_ref, w_ref, inv_ref, out_ref, sal_ref, sbuf, wbuf, place, sblk, m, gat, outv,
                xs_send, xs_recv, xw_send, xw_recv, up_send, up_recv, dn_send, dn_recv, pr_send, pr_recv,
                gu_send, gu_recv, gd_send, gd_recv, gp_send, gp_recv, out_sem):
    n_row, n_col = lax.axis_size("row"), lax.axis_size("col")
    n_z = n_row // 2
    rows, width = w_ref.shape
    n = idx_ref.shape[1]
    row, col = lax.axis_index("row"), lax.axis_index("col")
    z, core = row // 2, lax.rem(row, 2)
    up = lax.rem(row + 2, n_row)
    down = lax.rem(row + n_row - 2, n_row)
    partner = row + 1 - 2 * core

    barrier = pltpu.get_barrier_semaphore()
    for k in range(1, n_col):
        pl.semaphore_signal(barrier, inc=1, device_id={"row": row, "col": lax.rem(col + k, n_col)}, device_id_type=MESH_ID)
    for other in (up, down, partner):
        pl.semaphore_signal(barrier, inc=1, device_id={"row": other, "col": col}, device_id_type=MESH_ID)

    idx = idx_ref[...]
    anchor = col * width
    start = jnp.sum(jnp.where(idx < anchor, 1.0, 0.0), axis=1, keepdims=True)
    own = jnp.where((idx >= anchor) & (idx < anchor + width), 1.0, 0.0)
    high = idx // 256
    low = idx - high * 256
    sub8 = lax.broadcasted_iota(jnp.int32, (8, n), 0)
    facts = jnp.where(sub8 == 0, high.astype(F32), jnp.where(sub8 == 1, low.astype(F32), jnp.where(sub8 == 2, own, 0.0)))
    at = lax.broadcasted_iota(jnp.int32, (n, LANES), 0).astype(F32)
    slot = lax.broadcasted_iota(jnp.int32, (n, LANES), 1).astype(F32)
    window = jnp.where(at == slot + start, 1.0, 0.0).astype(BF16)
    picked = jnp.dot(facts.astype(BF16), window, preferred_element_type=F32)
    local = jnp.where(picked[2:3, :] > 0.5, picked[0:1, :] * 256.0 + picked[1:2, :] - anchor.astype(F32), -1.0)
    column = lax.broadcasted_iota(jnp.int32, (width, LANES), 0).astype(F32)
    picker = jnp.where(column == local, 1.0, 0.0).astype(BF16)

    ih, im, il = split3(inv_ref[...])
    part = inv_ref.shape[0]
    gat[0, 0, core] = ih
    gat[1, 0, core] = im
    three = jnp.dot(jnp.concatenate([ih, im, il], axis=0), picker, preferred_element_type=F32)
    sbuf[col] = three[0:part] + three[part:2 * part] + three[2 * part:3 * part]
    wbuf[col] = jnp.dot(w_ref[...], picker, preferred_element_type=F32).astype(BF16)

    pl.semaphore_wait(barrier, n_col + 2)
    ups, downs = n_z // 2, n_z - 1 - n_z // 2
    sent = []

    def push(p, block, landing, target_row, send_sem, recv_sem):
        c = pltpu.make_async_remote_copy(gat.at[p, block % n_z, core], gat.at[p, landing % n_z, core], send_sem, recv_sem,
                                         device_id={"row": target_row, "col": col}, device_id_type=MESH_ID)
        c.start()
        return c
    s_copies, w_copies = [], []
    for k in range(1, n_col):
        target = {"row": row, "col": lax.rem(col + k, n_col)}
        c = pltpu.make_async_remote_copy(sbuf.at[col], sbuf.at[col], xs_send.at[k], xs_recv.at[k], device_id=target, device_id_type=MESH_ID)
        c.start()
        s_copies.append(c)

    def give_w(k):
        target = {"row": row, "col": lax.rem(col + k, n_col)}
        c = pltpu.make_async_remote_copy(wbuf.at[col], wbuf.at[col], xw_send.at[k], xw_recv.at[k], device_id=target, device_id_type=MESH_ID)
        c.start()
        w_copies.append(c)

    fly_up, fly_dn, mates = {}, {}, []
    for p in range(2):
        fly_up[p] = push(p, 0, -1, up, gu_send.at[p, 0], gu_recv.at[p, 0])
        fly_dn[p] = push(p, 0, 1, down, gd_send.at[p, 0], gd_recv.at[p, 0])
        mates.append(push(p, 0, 0, partner, gp_send.at[p, 0], gp_recv.at[p, 0]))

    def service(piece):
        s, p = piece // 2 + 1, piece % 2
        fly_up[p].wait()
        if s < ups:
            fly_up[p] = push(p, -s, -s - 1, up, gu_send.at[p, s], gu_recv.at[p, s])
        if s <= downs:
            fly_dn[p].wait()
            if s < downs:
                fly_dn[p] = push(p, s, s + 1, down, gd_send.at[p, s], gd_recv.at[p, s])
        mates.append(push(p, -s, -s, partner, gp_send.at[p, s], gp_recv.at[p, s]))
        if s <= downs:
            mates.append(push(p, s, s, partner, gp_send.at[p, ups + s], gp_recv.at[p, ups + s]))

    shard = lax.broadcasted_iota(jnp.int32, (n_col, n), 0)
    starts = jnp.sum(jnp.where(idx < shard * width, 1.0, 0.0), axis=1, keepdims=True)
    mine = (idx >= shard * width) & (idx < (shard + 1) * width)
    base = jnp.sum(jnp.where(mine, (shard * LANES).astype(F32) - starts, 0.0), axis=0, keepdims=True)
    slot_of = base + lax.broadcasted_iota(jnp.int32, (1, n), 1).astype(F32)
    slot_of = pltpu.roll(jnp.broadcast_to(slot_of, (8, n)), lax.rem(n - BLOCK * z, n), 1)[0:1]
    m[...] = jnp.zeros_like(m)
    for c in range(n_col):
        q = lax.broadcasted_iota(jnp.int32, (LANES, n), 0).astype(F32) + float(c * LANES)
        place[c * LANES:(c + 1) * LANES, :] = jnp.where(q == slot_of, 1.0, 0.0).astype(BF16)

    for c in s_copies:
        c.wait()
    joined = jnp.concatenate([sbuf[c] for c in range(n_col)], axis=1)
    jh, jm, jl = split3(joined)
    three = jnp.dot(jnp.concatenate([jh, jm, jl], axis=0), place[...], preferred_element_type=F32)
    sblk[0, core] = three[0:part] + three[part:2 * part] + three[2 * part:3 * part]

    def send(block, landing, target_row, send_sem, recv_sem):
        c = pltpu.make_async_remote_copy(sblk.at[block % n_z, core], sblk.at[landing % n_z, core], send_sem, recv_sem,
                                         device_id={"row": target_row, "col": col}, device_id_type=MESH_ID)
        c.start()
        return c

    def turned(block):
        both = jnp.concatenate([sblk[block % n_z, 0], sblk[block % n_z, 1]], axis=0)
        shift = BLOCK * (block % n_z)
        return pltpu.roll(both, shift, 1) if shift else both

    done = [0]

    def serve(count):
        for _ in range(count):
            if done[0] < 2 * ups:
                service(done[0])
                done[0] += 1

    fly_s_up = send(0, -1, up, up_send.at[0], up_recv.at[0])
    fly_s_dn = send(0, 1, down, dn_send.at[0], dn_recv.at[0])
    fresh = {0: [send(0, 0, partner, pr_send.at[0], pr_recv.at[0])]}
    column_at = lax.broadcasted_iota(jnp.int32, (2 * BLOCK, n), 1)

    def take(s):
        for c in fresh[s]:
            c.wait()
        if s == 0:
            m[0:BLOCK, :] = pivot(turned(0), 0)[1]
            serve(MID[s])
            return
        blocks = [n_z - s, s] if s <= downs else [n_z - s]
        arrived = jnp.concatenate([turned(b) for b in blocks], axis=0)
        count = arrived.shape[0]
        known = (column_at[0:count] < BLOCK * s) | (column_at[0:count] >= n - BLOCK * (s - 1))
        h, mid, low3 = split3(jnp.where(known, arrived, 0.0))
        stack = jnp.concatenate([h, mid, low3], axis=0)
        near = 4 * s <= n_z
        spans = [(0, n // 4), (3 * n // 4, n)] if near else [(0, n)]
        stack = jnp.concatenate([stack[:, a:b] for a, b in spans], axis=1)
        mh, mm, ml = split3(jnp.concatenate([m[a:b, :] for a, b in spans], axis=0))
        p1 = jnp.dot(stack, mh, preferred_element_type=F32)
        p2 = jnp.dot(stack[0:2 * count], mm, preferred_element_type=F32)
        p3 = jnp.dot(stack[0:count], ml, preferred_element_type=F32)
        caught = p1[0:count] + ((p1[count:2 * count] + p2[0:count]) + ((p1[2 * count:] + p2[count:]) + p3))
        arrived = jnp.where(known, 0.0, arrived) + caught
        first = arrived[0:BLOCK]
        low_end, high_end = BLOCK * s, n - BLOCK * (s - 1)
        kb = BLOCK * (n_z - s)
        right, new = pivot(first, kb)
        if s <= downs:
            second = reduced(arrived[BLOCK:], kb, right)
        m[0:low_end, :] = reduced(m[0:low_end, :], kb, right)
        if high_end < n:
            m[high_end:n, :] = reduced(m[high_end:n, :], kb, right)
        m[kb:kb + BLOCK, :] = new
        serve(MID[s])
        if s <= downs:
            right, new = pivot(second, BLOCK * s)
            m[0:low_end, :] = reduced(m[0:low_end, :], BLOCK * s, right)
            m[kb:n, :] = reduced(m[kb:n, :], BLOCK * s, right)
            m[BLOCK * s:BLOCK * s + BLOCK, :] = new

    for s in range(1, ups + 1):
        fly_s_up.wait()
        if s < ups:
            fly_s_up = send(-s, -s - 1, up, up_send.at[s], up_recv.at[s])
        if s <= downs:
            fly_s_dn.wait()
            if s < downs:
                fly_s_dn = send(s, s + 1, down, dn_send.at[s], dn_recv.at[s])
        fresh[s] = [send(-s, -s, partner, pr_send.at[s], pr_recv.at[s])]
        if s <= downs:
            fresh[s].append(send(s, s, partner, pr_send.at[ups + s], pr_recv.at[ups + s]))
        serve(PACE[s])
        for k in range((s - 1) * (n_col - 1) // ups, s * (n_col - 1) // ups):
            give_w(k + 1)
        take(s - 1)
    take(ups)
    for c in w_copies:
        c.wait()
    wj = jnp.concatenate([wbuf[c] for c in range(n_col)], axis=1)
    chosen = jnp.dot(wj, place[...], preferred_element_type=F32)
    picked_w = chosen.astype(BF16)
    mh, mm, ml = split3(m[...])
    solved = jnp.dot(picked_w, mh, preferred_element_type=F32) + (
        jnp.dot(picked_w, mm, preferred_element_type=F32) + jnp.dot(picked_w, ml, preferred_element_type=F32))
    hi = solved.astype(BF16)
    lo = (solved - hi.astype(F32)).astype(BF16)
    prod = solved * chosen
    folded = prod[:, 0:LANES]
    for t in range(1, n // LANES):
        folded = folded + prod[:, t * LANES:(t + 1) * LANES]
    sal_ref[...] = jnp.sum(folded.T, axis=0, keepdims=True) / (2.0 * n)
    serve(2 * ups)
    for c in mates:
        c.wait()
    both = jnp.concatenate([hi, lo], axis=0)
    units = width // 256
    cuts = [256 * (units * t // 4) for t in range(5)]
    stores = []
    for t in range(4):
        cs, tile = slice(cuts[t], cuts[t + 1]), cuts[t + 1] - cuts[t]
        gh = gat[0, :, :, :, cs].reshape(n, tile)
        gl = gat[1, :, :, :, cs].reshape(n, tile)
        a = jnp.dot(both, gh, preferred_element_type=F32)
        acc = a[0:rows] + a[rows:2 * rows] + jnp.dot(hi, gl, preferred_element_type=F32)
        outv[:, cs] = (w_ref[:, cs].astype(F32) - acc).astype(BF16)
        c = pltpu.make_async_copy(outv.at[:, cs], out_ref.at[:, cs], out_sem.at[t])
        c.start()
        stores.append(c)
    for c in stores:
        c.wait()


def step(idx, weight, inverse_rows, n_row, n_col):
    n = idx.shape[1]
    rows, width = weight.shape
    part = inverse_rows.shape[0]
    n_z = n_row // 2
    dma = pltpu.SemaphoreType.DMA
    vm = pl.BlockSpec(memory_space=pltpu.VMEM)
    return pl.pallas_call(
        step_kernel,
        out_shape=(jax.ShapeDtypeStruct((rows, width), BF16), jax.ShapeDtypeStruct((1, rows), F32)),
        in_specs=[vm] * 3,
        out_specs=(pl.BlockSpec(memory_space=pl.ANY), vm),
        scratch_shapes=[
            pltpu.VMEM((n_col, part, LANES), F32),
            pltpu.VMEM((n_col, rows, LANES), BF16),
            pltpu.VMEM((n_col * LANES, n), BF16),
            pltpu.VMEM((n_z, 2, part, n), F32),
            pltpu.VMEM((n, n), F32),
            pltpu.VMEM((2, n_z, 2, part, width), BF16),
            pltpu.VMEM((rows, width), BF16),
            dma((n_col,)), dma((n_col,)), dma((n_col,)), dma((n_col,)),
            dma((n_z,)), dma((n_z,)), dma((n_z,)), dma((n_z,)), dma((n_z,)), dma((n_z,)),
            dma((2, n_z)), dma((2, n_z)), dma((2, n_z)), dma((2, n_z)), dma((2, n_z)), dma((2, n_z)),
            dma((4,)),
        ],
        compiler_params=pltpu.CompilerParams(collective_id=0, has_side_effects=True, vmem_limit_bytes=60 << 20),
        name="step",
    )(idx, weight, inverse_rows)


def solution(mesh):
    n_row, n_col = mesh.shape["row"], mesh.shape["col"]

    def body(weight, inverse_rows, pruned_index):
        out, sal = step(pruned_index[None, :], weight, inverse_rows, n_row, n_col)
        return out, sal[0]

    return jax.shard_map(
        body,
        mesh=mesh,
        in_specs=(P("row", "col"), P("row", "col"), P()),
        out_specs=(P("row", "col"), P("row")),
        check_vma=False,
    )
```

```python
import functools

import jax
import jax.numpy as jnp
from jax import lax
from jax.experimental import pallas as pl
from jax.experimental.pallas import tpu as pltpu
from jax.sharding import PartitionSpec as P

F32, BF16 = jnp.float32, jnp.bfloat16
LANES = 128
BLOCK = 32
PACE = (2, 0, 1, 1, 1, 1, 1, 1, 1)
MID = (0, 1, 0, 1, 0, 1, 0, 1, 1)


def split3(x):
    hi = x.astype(BF16)
    r = x - hi.astype(F32)
    mid = r.astype(BF16)
    lo = (r - mid.astype(F32)).astype(BF16)
    return hi, mid, lo

def bsub(x, k):
    return jnp.broadcast_to(x[k:k+1, :], x.shape)

def inv8(cols):
    sub = lax.broadcasted_iota(jnp.int32, (8, 128), 0)
    for k in range(8):
        t = [bsub(c, k) for c in cols]
        r = 1.0 / t[k]
        ck = cols[k]
        new = []
        for j in range(8):
            if j == k:
                new.append(jnp.where(sub == k, r, -(ck * r)))
            else:
                new.append(jnp.where(sub == k, t[j] * r, cols[j] - (ck * t[j]) * r))
        cols = new
    return cols

def panel_gj(P, kb, nb, nt):
    lane = lax.broadcasted_iota(jnp.int32, (8, 128), 1)
    sub = lax.broadcasted_iota(jnp.int32, (8, 128), 0)
    for g in range(nb):
        col0 = kb + g * 8
        pt, l0 = col0 // 128, col0 % 128
        C = [[jnp.broadcast_to(P[i][pt][:, l0 + j:l0 + j + 1], (8, 128)) for j in range(8)] for i in range(nb)]
        Dinv = inv8(C[g])
        inside = (lane >= l0) & (lane < l0 + 8)
        eye = jnp.where(lane - l0 == sub, 1.0, 0.0)
        for i in range(nb):
            P[i][pt] = jnp.where(inside, eye if i == g else 0.0, P[i][pt])
        U = []
        for t in range(nt):
            acc = Dinv[0] * bsub(P[g][t], 0)
            for j in range(1, 8):
                acc = acc + Dinv[j] * bsub(P[g][t], j)
            U.append(acc)
        for t in range(nt):
            ub = [bsub(U[t], j) for j in range(8)]
            for i in range(nb):
                if i != g:
                    acc = P[i][t]
                    for j in range(8):
                        acc = acc - C[i][j] * ub[j]
                    P[i][t] = acc
            P[g][t] = U[t]
    return P


def stack_left(x):
    h, m, l = split3(x)
    return jnp.concatenate([h, h, m, h, m, l], axis=1)


def pivot(rows, kb):
    n = rows.shape[1]
    nb, nt = BLOCK // 8, n // LANES
    lane = lax.broadcasted_iota(jnp.int32, (8, LANES), 1)
    sub = lax.broadcasted_iota(jnp.int32, (8, LANES), 0)
    P = [[rows[g * 8:g * 8 + 8, t * LANES:(t + 1) * LANES] for t in range(nt)] for g in range(nb)]
    P = panel_gj(P, kb, nb, nt)
    pt, l0 = kb // LANES, kb % LANES
    inside = (lane >= l0) & (lane < l0 + BLOCK)
    upd, new = [], []
    for g in range(nb):
        eye = jnp.where(lane - l0 == sub + g * 8, 1.0, 0.0)
        urow = [jnp.where(inside, eye - x, x) if t == pt else x for t, x in enumerate(P[g])]
        nrow = [jnp.where(inside, x, -x) if t == pt else -x for t, x in enumerate(P[g])]
        upd.append(jnp.concatenate(urow, axis=1))
        new.append(jnp.concatenate(nrow, axis=1))
    uh, um, ul = split3(jnp.concatenate(upd, axis=0))
    return jnp.concatenate([uh, um, uh, ul, um, uh], axis=0), jnp.concatenate(new, axis=0)


def reduced(x, kb, right):
    return x - jnp.dot(stack_left(x[:, kb:kb + BLOCK]), right, preferred_element_type=F32)


MESH_ID = pl.DeviceIdType.MESH


def step_kernel(idx_ref, w_hbm, inv_ref, out_ref, sal_ref, sbuf, wbuf, place, sblk, m, gat, outv, w_ref, load_sem,
                xs_send, xs_recv, xw_send, xw_recv, up_send, up_recv, dn_send, dn_recv, pr_send, pr_recv,
                gu_send, gu_recv, gd_send, gd_recv, gp_send, gp_recv, out_sem):
    n_row, n_col = lax.axis_size("row"), lax.axis_size("col")
    n_z = n_row // 2
    rows, width = w_hbm.shape
    n = idx_ref.shape[1]
    row, col = lax.axis_index("row"), lax.axis_index("col")
    z, core = row // 2, lax.rem(row, 2)
    up = lax.rem(row + 2, n_row)
    down = lax.rem(row + n_row - 2, n_row)
    partner = row + 1 - 2 * core

    barrier = pltpu.get_barrier_semaphore()
    for k in range(1, n_col):
        pl.semaphore_signal(barrier, inc=1, device_id={"row": row, "col": lax.rem(col + k, n_col)}, device_id_type=MESH_ID)
    for other in (up, down, partner):
        pl.semaphore_signal(barrier, inc=1, device_id={"row": other, "col": col}, device_id_type=MESH_ID)

    load = pltpu.make_async_copy(w_hbm, w_ref, load_sem)
    load.start()
    idx = idx_ref[...]
    anchor = col * width
    start = jnp.sum(jnp.where(idx < anchor, 1.0, 0.0), axis=1, keepdims=True)
    own = jnp.where((idx >= anchor) & (idx < anchor + width), 1.0, 0.0)
    high = idx // 256
    low = idx - high * 256
    sub8 = lax.broadcasted_iota(jnp.int32, (8, n), 0)
    facts = jnp.where(sub8 == 0, high.astype(F32), jnp.where(sub8 == 1, low.astype(F32), jnp.where(sub8 == 2, own, 0.0)))
    at = lax.broadcasted_iota(jnp.int32, (n, LANES), 0).astype(F32)
    slot = lax.broadcasted_iota(jnp.int32, (n, LANES), 1).astype(F32)
    window = jnp.where(at == slot + start, 1.0, 0.0).astype(BF16)
    picked = jnp.dot(facts.astype(BF16), window, preferred_element_type=F32)
    local = jnp.where(picked[2:3, :] > 0.5, picked[0:1, :] * 256.0 + picked[1:2, :] - anchor.astype(F32), -1.0)
    column = lax.broadcasted_iota(jnp.int32, (width, LANES), 0).astype(F32)
    picker = jnp.where(column == local, 1.0, 0.0).astype(BF16)

    ih, im, il = split3(inv_ref[...])
    part = inv_ref.shape[0]
    gat[0, 0, core] = ih
    gat[1, 0, core] = im
    three = jnp.dot(jnp.concatenate([ih, im, il], axis=0), picker, preferred_element_type=F32)
    sbuf[col] = three[0:part] + three[part:2 * part] + three[2 * part:3 * part]
    load.wait()
    wbuf[col] = jnp.dot(w_ref[...], picker, preferred_element_type=F32).astype(BF16)

    pl.semaphore_wait(barrier, n_col + 2)
    ups, downs = n_z // 2, n_z - 1 - n_z // 2
    sent = []

    def push(p, block, landing, target_row, send_sem, recv_sem):
        c = pltpu.make_async_remote_copy(gat.at[p, block % n_z, core], gat.at[p, landing % n_z, core], send_sem, recv_sem,
                                         device_id={"row": target_row, "col": col}, device_id_type=MESH_ID)
        c.start()
        return c
    s_copies, w_copies = [], []
    for k in range(1, n_col):
        target = {"row": row, "col": lax.rem(col + k, n_col)}
        c = pltpu.make_async_remote_copy(sbuf.at[col], sbuf.at[col], xs_send.at[k], xs_recv.at[k], device_id=target, device_id_type=MESH_ID)
        c.start()
        s_copies.append(c)

    def give_w(k):
        target = {"row": row, "col": lax.rem(col + k, n_col)}
        c = pltpu.make_async_remote_copy(wbuf.at[col], wbuf.at[col], xw_send.at[k], xw_recv.at[k], device_id=target, device_id_type=MESH_ID)
        c.start()
        w_copies.append(c)

    fly_up, fly_dn, mates = {}, {}, []
    for p in range(2):
        fly_up[p] = push(p, 0, -1, up, gu_send.at[p, 0], gu_recv.at[p, 0])
        fly_dn[p] = push(p, 0, 1, down, gd_send.at[p, 0], gd_recv.at[p, 0])
        mates.append(push(p, 0, 0, partner, gp_send.at[p, 0], gp_recv.at[p, 0]))

    def service(piece):
        s, p = piece // 2 + 1, piece % 2
        if s < ups or p == 0:
            fly_up[p].wait()
            if s + 1 < ups or (s + 1 == ups and p == 0):
                fly_up[p] = push(p, -s, -s - 1, up, gu_send.at[p, s], gu_recv.at[p, s])
        if s < ups or p == 1:
            fly_dn[p].wait()
            if s + 1 < ups or (s + 1 == ups and p == 1):
                fly_dn[p] = push(p, s, s + 1, down, gd_send.at[p, s], gd_recv.at[p, s])
        mates.append(push(p, -s, -s, partner, gp_send.at[p, s], gp_recv.at[p, s]))
        if s < ups:
            mates.append(push(p, s, s, partner, gp_send.at[p, ups + s], gp_recv.at[p, ups + s]))

    shard = lax.broadcasted_iota(jnp.int32, (n_col, n), 0)
    starts = jnp.sum(jnp.where(idx < shard * width, 1.0, 0.0), axis=1, keepdims=True)
    mine = (idx >= shard * width) & (idx < (shard + 1) * width)
    base = jnp.sum(jnp.where(mine, (shard * LANES).astype(F32) - starts, 0.0), axis=0, keepdims=True)
    slot_of = base + lax.broadcasted_iota(jnp.int32, (1, n), 1).astype(F32)
    slot_of = pltpu.roll(jnp.broadcast_to(slot_of, (8, n)), lax.rem(n - BLOCK * z, n), 1)[0:1]
    m[...] = jnp.zeros_like(m)
    for c in range(n_col):
        q = lax.broadcasted_iota(jnp.int32, (LANES, n), 0).astype(F32) + float(c * LANES)
        place[c * LANES:(c + 1) * LANES, :] = jnp.where(q == slot_of, 1.0, 0.0).astype(BF16)

    for c in s_copies:
        c.wait()
    joined = jnp.concatenate([sbuf[c] for c in range(n_col)], axis=1)
    jh, jm, jl = split3(joined)
    three = jnp.dot(jnp.concatenate([jh, jm, jl], axis=0), place[...], preferred_element_type=F32)
    sblk[0, core] = three[0:part] + three[part:2 * part] + three[2 * part:3 * part]

    def send(block, landing, target_row, send_sem, recv_sem):
        c = pltpu.make_async_remote_copy(sblk.at[block % n_z, core], sblk.at[landing % n_z, core], send_sem, recv_sem,
                                         device_id={"row": target_row, "col": col}, device_id_type=MESH_ID)
        c.start()
        return c

    def turned(block):
        both = jnp.concatenate([sblk[block % n_z, 0], sblk[block % n_z, 1]], axis=0)
        shift = BLOCK * (block % n_z)
        return pltpu.roll(both, shift, 1) if shift else both

    done = [0]

    def serve(count):
        for _ in range(count):
            if done[0] < 2 * ups:
                service(done[0])
                done[0] += 1

    fly_s_up = send(0, -1, up, up_send.at[0], up_recv.at[0])
    fly_s_dn = send(0, 1, down, dn_send.at[0], dn_recv.at[0])
    fresh = {0: [send(0, 0, partner, pr_send.at[0], pr_recv.at[0])]}
    serve(PACE[0])
    column_at = lax.broadcasted_iota(jnp.int32, (2 * BLOCK, n), 1)

    def take(s):
        for c in fresh[s]:
            c.wait()
        if s == 0:
            m[0:BLOCK, :] = pivot(turned(0), 0)[1]
            serve(MID[s])
            return
        blocks = [n_z - s, s] if s <= downs else [n_z - s]
        arrived = jnp.concatenate([turned(b) for b in blocks], axis=0)
        count = arrived.shape[0]
        known = (column_at[0:count] < BLOCK * s) | (column_at[0:count] >= n - BLOCK * (s - 1))
        h, mid, low3 = split3(jnp.where(known, arrived, 0.0))
        stack = jnp.concatenate([h, mid, low3], axis=0)
        near = 4 * s <= n_z
        spans = [(0, n // 4), (3 * n // 4, n)] if near else [(0, n)]
        stack = jnp.concatenate([stack[:, a:b] for a, b in spans], axis=1)
        mh, mm, ml = split3(jnp.concatenate([m[a:b, :] for a, b in spans], axis=0))
        p1 = jnp.dot(stack, mh, preferred_element_type=F32)
        p2 = jnp.dot(stack[0:2 * count], mm, preferred_element_type=F32)
        p3 = jnp.dot(stack[0:count], ml, preferred_element_type=F32)
        caught = p1[0:count] + ((p1[count:2 * count] + p2[0:count]) + ((p1[2 * count:] + p2[count:]) + p3))
        arrived = jnp.where(known, 0.0, arrived) + caught
        first = arrived[0:BLOCK]
        low_end, high_end = BLOCK * s, n - BLOCK * (s - 1)
        kb = BLOCK * (n_z - s)
        right, new = pivot(first, kb)
        if s <= downs:
            second = reduced(arrived[BLOCK:], kb, right)
        m[0:low_end, :] = reduced(m[0:low_end, :], kb, right)
        if high_end < n:
            m[high_end:n, :] = reduced(m[high_end:n, :], kb, right)
        m[kb:kb + BLOCK, :] = new
        serve(MID[s])
        if s <= downs:
            right, new = pivot(second, BLOCK * s)
            m[0:low_end, :] = reduced(m[0:low_end, :], BLOCK * s, right)
            m[kb:n, :] = reduced(m[kb:n, :], BLOCK * s, right)
            m[BLOCK * s:BLOCK * s + BLOCK, :] = new

    for s in range(1, ups + 1):
        fly_s_up.wait()
        if s < ups:
            fly_s_up = send(-s, -s - 1, up, up_send.at[s], up_recv.at[s])
        if s <= downs:
            fly_s_dn.wait()
            if s < downs:
                fly_s_dn = send(s, s + 1, down, dn_send.at[s], dn_recv.at[s])
        fresh[s] = [send(-s, -s, partner, pr_send.at[s], pr_recv.at[s])]
        if s <= downs:
            fresh[s].append(send(s, s, partner, pr_send.at[ups + s], pr_recv.at[ups + s]))
        serve(PACE[s])
        for k in range((s - 1) * (n_col - 1) // ups, s * (n_col - 1) // ups):
            give_w(k + 1)
        take(s - 1)
    take(ups)
    for c in w_copies:
        c.wait()
    wj = jnp.concatenate([wbuf[c] for c in range(n_col)], axis=1)
    chosen = jnp.dot(wj, place[...], preferred_element_type=F32)
    picked_w = chosen.astype(BF16)
    mh, mm, ml = split3(m[...])
    solved = jnp.dot(picked_w, mh, preferred_element_type=F32) + (
        jnp.dot(picked_w, mm, preferred_element_type=F32) + jnp.dot(picked_w, ml, preferred_element_type=F32))
    hi = solved.astype(BF16)
    lo = (solved - hi.astype(F32)).astype(BF16)
    prod = solved * chosen
    folded = prod[:, 0:LANES]
    for t in range(1, n // LANES):
        folded = folded + prod[:, t * LANES:(t + 1) * LANES]
    sal_ref[...] = jnp.sum(folded.T, axis=0, keepdims=True) / (2.0 * n)
    serve(2 * ups)
    for c in mates:
        c.wait()
    both = jnp.concatenate([hi, lo], axis=0)
    units = width // 256
    cuts = [256 * (units * t // 4) for t in range(5)]
    stores = []
    for t in range(4):
        cs, tile = slice(cuts[t], cuts[t + 1]), cuts[t + 1] - cuts[t]
        gh = gat[0, :, :, :, cs].reshape(n, tile)
        gl = gat[1, :, :, :, cs].reshape(n, tile)
        a = jnp.dot(both, gh, preferred_element_type=F32)
        acc = a[0:rows] + a[rows:2 * rows] + jnp.dot(hi, gl, preferred_element_type=F32)
        outv[:, cs] = (w_ref[:, cs].astype(F32) - acc).astype(BF16)
        c = pltpu.make_async_copy(outv.at[:, cs], out_ref.at[:, cs], out_sem.at[t])
        c.start()
        stores.append(c)
    for c in stores:
        c.wait()


def step(idx, weight, inverse_rows, n_row, n_col):
    n = idx.shape[1]
    rows, width = weight.shape
    part = inverse_rows.shape[0]
    n_z = n_row // 2
    dma = pltpu.SemaphoreType.DMA
    vm = pl.BlockSpec(memory_space=pltpu.VMEM)
    return pl.pallas_call(
        step_kernel,
        out_shape=(jax.ShapeDtypeStruct((rows, width), BF16), jax.ShapeDtypeStruct((1, rows), F32)),
        in_specs=[vm, pl.BlockSpec(memory_space=pl.ANY), vm],
        out_specs=(pl.BlockSpec(memory_space=pl.ANY), vm),
        scratch_shapes=[
            pltpu.VMEM((n_col, part, LANES), F32),
            pltpu.VMEM((n_col, rows, LANES), BF16),
            pltpu.VMEM((n_col * LANES, n), BF16),
            pltpu.VMEM((n_z, 2, part, n), F32),
            pltpu.VMEM((n, n), F32),
            pltpu.VMEM((2, n_z, 2, part, width), BF16),
            pltpu.VMEM((rows, width), BF16),
            pltpu.VMEM((rows, width), BF16),
            dma,
            dma((n_col,)), dma((n_col,)), dma((n_col,)), dma((n_col,)),
            dma((n_z,)), dma((n_z,)), dma((n_z,)), dma((n_z,)), dma((n_z,)), dma((n_z,)),
            dma((2, n_z)), dma((2, n_z)), dma((2, n_z)), dma((2, n_z)), dma((2, n_z)), dma((2, n_z)),
            dma((4,)),
        ],
        compiler_params=pltpu.CompilerParams(collective_id=0, has_side_effects=True, vmem_limit_bytes=60 << 20),
        name="step",
    )(idx, weight, inverse_rows)


def settle_kernel(o_ref, s_ref, out_ref, sal_ref, buf, in_sem, out_sem):
    parts = buf.shape[0]
    rows = buf.shape[1]
    ins = [pltpu.make_async_copy(o_ref.at[i * rows:(i + 1) * rows, :], buf.at[i], in_sem.at[i]) for i in range(parts)]
    outs = [pltpu.make_async_copy(buf.at[i], out_ref.at[i * rows:(i + 1) * rows, :], out_sem.at[i]) for i in range(parts)]
    for c in ins:
        c.start()
    sal_ref[...] = s_ref[...]
    for i in range(parts):
        ins[i].wait()
        outs[i].start()
    for c in outs:
        c.wait()


def settle(out, sal, parts=8):
    anyspace, vm = pl.BlockSpec(memory_space=pl.ANY), pl.BlockSpec(memory_space=pltpu.VMEM)
    return pl.pallas_call(
        settle_kernel,
        out_shape=(jax.ShapeDtypeStruct(out.shape, out.dtype), jax.ShapeDtypeStruct(sal.shape, sal.dtype)),
        in_specs=[anyspace, vm],
        out_specs=(anyspace, vm),
        scratch_shapes=[pltpu.VMEM((parts, out.shape[0] // parts, out.shape[1]), out.dtype),
                        pltpu.SemaphoreType.DMA((parts,)), pltpu.SemaphoreType.DMA((parts,))],
        name="settle",
    )(out, sal)


def solution(mesh):
    n_row, n_col = mesh.shape["row"], mesh.shape["col"]

    def body(weight, inverse_rows, pruned_index):
        out, sal = settle(*step(pruned_index[None, :], weight, inverse_rows, n_row, n_col))
        return out, sal[0]

    return jax.shard_map(
        body,
        mesh=mesh,
        in_specs=(P("row", "col"), P("row", "col"), P()),
        out_specs=(P("row", "col"), P("row")),
        check_vma=False,
    )
```

```python
import functools

import jax
import jax.numpy as jnp
from jax import lax
from jax.experimental import pallas as pl
from jax.experimental.pallas import tpu as pltpu
from jax.sharding import PartitionSpec as P

F32, BF16 = jnp.float32, jnp.bfloat16
LANES = 128
BLOCK = 32
PACE = (2, 0, 1, 1, 1, 1, 1, 1, 1)
MID = (0, 1, 0, 1, 1, 1, 0, 1, 1)


def split3(x):
    hi = x.astype(BF16)
    r = x - hi.astype(F32)
    mid = r.astype(BF16)
    lo = (r - mid.astype(F32)).astype(BF16)
    return hi, mid, lo

def bsub(x, k):
    return jnp.broadcast_to(x[k:k+1, :], x.shape)

def inv8(cols):
    sub = lax.broadcasted_iota(jnp.int32, (8, 128), 0)
    for k in range(8):
        t = [bsub(c, k) for c in cols]
        r = 1.0 / t[k]
        ck = cols[k]
        new = []
        for j in range(8):
            if j == k:
                new.append(jnp.where(sub == k, r, -(ck * r)))
            else:
                new.append(jnp.where(sub == k, t[j] * r, cols[j] - (ck * t[j]) * r))
        cols = new
    return cols

def panel_gj(P, kb, nb, nt):
    lane = lax.broadcasted_iota(jnp.int32, (8, 128), 1)
    sub = lax.broadcasted_iota(jnp.int32, (8, 128), 0)
    for g in range(nb):
        col0 = kb + g * 8
        pt, l0 = col0 // 128, col0 % 128
        C = [[jnp.broadcast_to(P[i][pt][:, l0 + j:l0 + j + 1], (8, 128)) for j in range(8)] for i in range(nb)]
        Dinv = inv8(C[g])
        inside = (lane >= l0) & (lane < l0 + 8)
        eye = jnp.where(lane - l0 == sub, 1.0, 0.0)
        for i in range(nb):
            P[i][pt] = jnp.where(inside, eye if i == g else 0.0, P[i][pt])
        U = []
        for t in range(nt):
            acc = Dinv[0] * bsub(P[g][t], 0)
            for j in range(1, 8):
                acc = acc + Dinv[j] * bsub(P[g][t], j)
            U.append(acc)
        for t in range(nt):
            ub = [bsub(U[t], j) for j in range(8)]
            for i in range(nb):
                if i != g:
                    acc = P[i][t]
                    for j in range(8):
                        acc = acc - C[i][j] * ub[j]
                    P[i][t] = acc
            P[g][t] = U[t]
    return P


def stack_left(x):
    h, m, l = split3(x)
    return jnp.concatenate([h, h, m, h, m, l], axis=1)


def pivot(rows, kb):
    n = rows.shape[1]
    nb, nt = BLOCK // 8, n // LANES
    lane = lax.broadcasted_iota(jnp.int32, (8, LANES), 1)
    sub = lax.broadcasted_iota(jnp.int32, (8, LANES), 0)
    P = [[rows[g * 8:g * 8 + 8, t * LANES:(t + 1) * LANES] for t in range(nt)] for g in range(nb)]
    P = panel_gj(P, kb, nb, nt)
    pt, l0 = kb // LANES, kb % LANES
    inside = (lane >= l0) & (lane < l0 + BLOCK)
    upd, new = [], []
    for g in range(nb):
        eye = jnp.where(lane - l0 == sub + g * 8, 1.0, 0.0)
        urow = [jnp.where(inside, eye - x, x) if t == pt else x for t, x in enumerate(P[g])]
        nrow = [jnp.where(inside, x, -x) if t == pt else -x for t, x in enumerate(P[g])]
        upd.append(jnp.concatenate(urow, axis=1))
        new.append(jnp.concatenate(nrow, axis=1))
    uh, um, ul = split3(jnp.concatenate(upd, axis=0))
    return jnp.concatenate([uh, um, uh, ul, um, uh], axis=0), jnp.concatenate(new, axis=0)


def reduced(x, kb, right):
    return x - jnp.dot(stack_left(x[:, kb:kb + BLOCK]), right, preferred_element_type=F32)


MESH_ID = pl.DeviceIdType.MESH


def step_kernel(idx_ref, w_hbm, inv_ref, out_ref, sal_ref, sbuf, wbuf, place, sblk, m, gat, outv, w_ref, load_sem,
                xs_send, xs_recv, xw_send, xw_recv, up_send, up_recv, dn_send, dn_recv, pr_send, pr_recv,
                gu_send, gu_recv, gd_send, gd_recv, gp_send, gp_recv, out_sem):
    n_row, n_col = lax.axis_size("row"), lax.axis_size("col")
    n_z = n_row // 2
    rows, width = w_hbm.shape
    n = idx_ref.shape[1]
    row, col = lax.axis_index("row"), lax.axis_index("col")
    z, core = row // 2, lax.rem(row, 2)
    up = lax.rem(row + 2, n_row)
    down = lax.rem(row + n_row - 2, n_row)
    partner = row + 1 - 2 * core

    barrier = pltpu.get_barrier_semaphore()
    for k in range(1, n_col):
        pl.semaphore_signal(barrier, inc=1, device_id={"row": row, "col": lax.rem(col + k, n_col)}, device_id_type=MESH_ID)
    for other in (up, down, partner):
        pl.semaphore_signal(barrier, inc=1, device_id={"row": other, "col": col}, device_id_type=MESH_ID)

    load = pltpu.make_async_copy(w_hbm, w_ref, load_sem)
    load.start()
    idx = idx_ref[...]
    anchor = col * width
    start = jnp.sum(jnp.where(idx < anchor, 1.0, 0.0), axis=1, keepdims=True)
    own = jnp.where((idx >= anchor) & (idx < anchor + width), 1.0, 0.0)
    high = idx // 256
    low = idx - high * 256
    sub8 = lax.broadcasted_iota(jnp.int32, (8, n), 0)
    facts = jnp.where(sub8 == 0, high.astype(F32), jnp.where(sub8 == 1, low.astype(F32), jnp.where(sub8 == 2, own, 0.0)))
    at = lax.broadcasted_iota(jnp.int32, (n, LANES), 0).astype(F32)
    slot = lax.broadcasted_iota(jnp.int32, (n, LANES), 1).astype(F32)
    window = jnp.where(at == slot + start, 1.0, 0.0).astype(BF16)
    picked = jnp.dot(facts.astype(BF16), window, preferred_element_type=F32)
    local = jnp.where(picked[2:3, :] > 0.5, picked[0:1, :] * 256.0 + picked[1:2, :] - anchor.astype(F32), -1.0)
    column = lax.broadcasted_iota(jnp.int32, (width, LANES), 0).astype(F32)
    picker = jnp.where(column == local, 1.0, 0.0).astype(BF16)

    ih, im, il = split3(inv_ref[...])
    part = inv_ref.shape[0]
    gat[0, 0, core] = ih
    gat[1, 0, core] = im
    three = jnp.dot(jnp.concatenate([ih, im, il], axis=0), picker, preferred_element_type=F32)
    sbuf[col] = three[0:part] + three[part:2 * part] + three[2 * part:3 * part]
    load.wait()
    wbuf[col] = jnp.dot(w_ref[...], picker, preferred_element_type=F32).astype(BF16)

    pl.semaphore_wait(barrier, n_col + 2)
    ups, downs = n_z // 2, n_z - 1 - n_z // 2
    sent = []

    def push(p, block, landing, target_row, send_sem, recv_sem):
        c = pltpu.make_async_remote_copy(gat.at[p, block % n_z, core], gat.at[p, landing % n_z, core], send_sem, recv_sem,
                                         device_id={"row": target_row, "col": col}, device_id_type=MESH_ID)
        c.start()
        return c
    s_copies, w_copies = [], []
    for k in range(1, n_col):
        target = {"row": row, "col": lax.rem(col + k, n_col)}
        c = pltpu.make_async_remote_copy(sbuf.at[col], sbuf.at[col], xs_send.at[k], xs_recv.at[k], device_id=target, device_id_type=MESH_ID)
        c.start()
        s_copies.append(c)

    def give_w(k):
        target = {"row": row, "col": lax.rem(col + k, n_col)}
        c = pltpu.make_async_remote_copy(wbuf.at[col], wbuf.at[col], xw_send.at[k], xw_recv.at[k], device_id=target, device_id_type=MESH_ID)
        c.start()
        w_copies.append(c)

    fly_up, fly_dn, mates = {}, {}, []
    for p in range(2):
        fly_up[p] = push(p, 0, -1, up, gu_send.at[p, 0], gu_recv.at[p, 0])
        fly_dn[p] = push(p, 0, 1, down, gd_send.at[p, 0], gd_recv.at[p, 0])
        mates.append(push(p, 0, 0, partner, gp_send.at[p, 0], gp_recv.at[p, 0]))

    def service(piece):
        s, p = piece // 2 + 1, piece % 2
        if s < ups or p == 0:
            fly_up[p].wait()
            if s + 1 < ups or (s + 1 == ups and p == 0):
                fly_up[p] = push(p, -s, -s - 1, up, gu_send.at[p, s], gu_recv.at[p, s])
        if s < ups or p == 1:
            fly_dn[p].wait()
            if s + 1 < ups or (s + 1 == ups and p == 1):
                fly_dn[p] = push(p, s, s + 1, down, gd_send.at[p, s], gd_recv.at[p, s])
        mates.append(push(p, -s, -s, partner, gp_send.at[p, s], gp_recv.at[p, s]))
        if s < ups:
            mates.append(push(p, s, s, partner, gp_send.at[p, ups + s], gp_recv.at[p, ups + s]))

    shard = lax.broadcasted_iota(jnp.int32, (n_col, n), 0)
    starts = jnp.sum(jnp.where(idx < shard * width, 1.0, 0.0), axis=1, keepdims=True)
    mine = (idx >= shard * width) & (idx < (shard + 1) * width)
    base = jnp.sum(jnp.where(mine, (shard * LANES).astype(F32) - starts, 0.0), axis=0, keepdims=True)
    slot_of = base + lax.broadcasted_iota(jnp.int32, (1, n), 1).astype(F32)
    slot_of = pltpu.roll(jnp.broadcast_to(slot_of, (8, n)), lax.rem(n - BLOCK * z, n), 1)[0:1]
    m[...] = jnp.zeros_like(m)
    for c in range(n_col):
        q = lax.broadcasted_iota(jnp.int32, (LANES, n), 0).astype(F32) + float(c * LANES)
        place[c * LANES:(c + 1) * LANES, :] = jnp.where(q == slot_of, 1.0, 0.0).astype(BF16)

    for c in s_copies:
        c.wait()
    joined = jnp.concatenate([sbuf[c] for c in range(n_col)], axis=1)
    jh, jm, jl = split3(joined)
    three = jnp.dot(jnp.concatenate([jh, jm, jl], axis=0), place[...], preferred_element_type=F32)
    sblk[0, core] = three[0:part] + three[part:2 * part] + three[2 * part:3 * part]

    def send(block, landing, target_row, send_sem, recv_sem):
        c = pltpu.make_async_remote_copy(sblk.at[block % n_z, core], sblk.at[landing % n_z, core], send_sem, recv_sem,
                                         device_id={"row": target_row, "col": col}, device_id_type=MESH_ID)
        c.start()
        return c

    def turned(block):
        both = jnp.concatenate([sblk[block % n_z, 0], sblk[block % n_z, 1]], axis=0)
        shift = BLOCK * (block % n_z)
        return pltpu.roll(both, shift, 1) if shift else both

    done = [0]

    def serve(count):
        for _ in range(count):
            if done[0] < 2 * ups:
                service(done[0])
                done[0] += 1

    fly_s_up = send(0, -1, up, up_send.at[0], up_recv.at[0])
    fly_s_dn = send(0, 1, down, dn_send.at[0], dn_recv.at[0])
    fresh = {0: [send(0, 0, partner, pr_send.at[0], pr_recv.at[0])]}
    serve(PACE[0])
    column_at = lax.broadcasted_iota(jnp.int32, (2 * BLOCK, n), 1)

    def take(s):
        for c in fresh[s]:
            c.wait()
        if s == 0:
            m[0:BLOCK, :] = pivot(turned(0), 0)[1]
            serve(MID[s])
            return
        blocks = [n_z - s, s] if s <= downs else [n_z - s]
        arrived = jnp.concatenate([turned(b) for b in blocks], axis=0)
        count = arrived.shape[0]
        known = (column_at[0:count] < BLOCK * s) | (column_at[0:count] >= n - BLOCK * (s - 1))
        h, mid, low3 = split3(jnp.where(known, arrived, 0.0))
        stack = jnp.concatenate([h, mid, low3], axis=0)
        near = 4 * s <= n_z
        spans = [(0, n // 4), (3 * n // 4, n)] if near else [(0, n)]
        stack = jnp.concatenate([stack[:, a:b] for a, b in spans], axis=1)
        mh, mm, ml = split3(jnp.concatenate([m[a:b, :] for a, b in spans], axis=0))
        p1 = jnp.dot(stack, mh, preferred_element_type=F32)
        p2 = jnp.dot(stack[0:2 * count], mm, preferred_element_type=F32)
        p3 = jnp.dot(stack[0:count], ml, preferred_element_type=F32)
        caught = p1[0:count] + ((p1[count:2 * count] + p2[0:count]) + ((p1[2 * count:] + p2[count:]) + p3))
        arrived = jnp.where(known, 0.0, arrived) + caught
        first = arrived[0:BLOCK]
        low_end, high_end = BLOCK * s, n - BLOCK * (s - 1)
        kb = BLOCK * (n_z - s)
        right, new = pivot(first, kb)
        if s <= downs:
            second = reduced(arrived[BLOCK:], kb, right)
        m[0:low_end, :] = reduced(m[0:low_end, :], kb, right)
        if high_end < n:
            m[high_end:n, :] = reduced(m[high_end:n, :], kb, right)
        m[kb:kb + BLOCK, :] = new
        serve(MID[s])
        if s <= downs:
            right, new = pivot(second, BLOCK * s)
            m[0:low_end, :] = reduced(m[0:low_end, :], BLOCK * s, right)
            m[kb:n, :] = reduced(m[kb:n, :], BLOCK * s, right)
            m[BLOCK * s:BLOCK * s + BLOCK, :] = new

    for s in range(1, ups + 1):
        fly_s_up.wait()
        if s < ups:
            fly_s_up = send(-s, -s - 1, up, up_send.at[s], up_recv.at[s])
        if s <= downs:
            fly_s_dn.wait()
            if s < downs:
                fly_s_dn = send(s, s + 1, down, dn_send.at[s], dn_recv.at[s])
        fresh[s] = [send(-s, -s, partner, pr_send.at[s], pr_recv.at[s])]
        if s <= downs:
            fresh[s].append(send(s, s, partner, pr_send.at[ups + s], pr_recv.at[ups + s]))
        serve(PACE[s])
        for k in range((s - 1) * (n_col - 1) // ups, s * (n_col - 1) // ups):
            give_w(k + 1)
        take(s - 1)
    take(ups)
    for c in w_copies:
        c.wait()
    wj = jnp.concatenate([wbuf[c] for c in range(n_col)], axis=1)
    chosen = jnp.dot(wj, place[...], preferred_element_type=F32)
    picked_w = chosen.astype(BF16)
    mh, mm, ml = split3(m[...])
    solved = jnp.dot(picked_w, mh, preferred_element_type=F32) + (
        jnp.dot(picked_w, mm, preferred_element_type=F32) + jnp.dot(picked_w, ml, preferred_element_type=F32))
    hi = solved.astype(BF16)
    lo = (solved - hi.astype(F32)).astype(BF16)
    prod = solved * chosen
    folded = prod[:, 0:LANES]
    for t in range(1, n // LANES):
        folded = folded + prod[:, t * LANES:(t + 1) * LANES]
    sal_ref[...] = jnp.sum(folded.T, axis=0, keepdims=True) / (2.0 * n)
    serve(2 * ups)
    for c in mates:
        c.wait()
    both = jnp.concatenate([hi, lo], axis=0)
    units = width // 256
    cuts = [256 * (units * t // 4) for t in range(5)]
    stores = []
    for t in range(4):
        cs, tile = slice(cuts[t], cuts[t + 1]), cuts[t + 1] - cuts[t]
        gh = gat[0, :, :, :, cs].reshape(n, tile)
        gl = gat[1, :, :, :, cs].reshape(n, tile)
        a = jnp.dot(both, gh, preferred_element_type=F32)
        acc = a[0:rows] + a[rows:2 * rows] + jnp.dot(hi, gl, preferred_element_type=F32)
        outv[:, cs] = (w_ref[:, cs].astype(F32) - acc).astype(BF16)
        c = pltpu.make_async_copy(outv.at[:, cs], out_ref.at[:, cs], out_sem.at[t])
        c.start()
        stores.append(c)
    for c in stores:
        c.wait()


def step(idx, weight, inverse_rows, n_row, n_col):
    n = idx.shape[1]
    rows, width = weight.shape
    part = inverse_rows.shape[0]
    n_z = n_row // 2
    dma = pltpu.SemaphoreType.DMA
    vm = pl.BlockSpec(memory_space=pltpu.VMEM)
    return pl.pallas_call(
        step_kernel,
        out_shape=(jax.ShapeDtypeStruct((rows, width), BF16), jax.ShapeDtypeStruct((1, rows), F32)),
        in_specs=[vm, pl.BlockSpec(memory_space=pl.ANY), vm],
        out_specs=(pl.BlockSpec(memory_space=pl.ANY), vm),
        scratch_shapes=[
            pltpu.VMEM((n_col, part, LANES), F32),
            pltpu.VMEM((n_col, rows, LANES), BF16),
            pltpu.VMEM((n_col * LANES, n), BF16),
            pltpu.VMEM((n_z, 2, part, n), F32),
            pltpu.VMEM((n, n), F32),
            pltpu.VMEM((2, n_z, 2, part, width), BF16),
            pltpu.VMEM((rows, width), BF16),
            pltpu.VMEM((rows, width), BF16),
            dma,
            dma((n_col,)), dma((n_col,)), dma((n_col,)), dma((n_col,)),
            dma((n_z,)), dma((n_z,)), dma((n_z,)), dma((n_z,)), dma((n_z,)), dma((n_z,)),
            dma((2, n_z)), dma((2, n_z)), dma((2, n_z)), dma((2, n_z)), dma((2, n_z)), dma((2, n_z)),
            dma((4,)),
        ],
        compiler_params=pltpu.CompilerParams(collective_id=0, has_side_effects=True, vmem_limit_bytes=60 << 20),
        name="step",
    )(idx, weight, inverse_rows)


def settle_kernel(o_ref, s_ref, out_ref, sal_ref, buf, in_sem, out_sem):
    parts = buf.shape[0]
    rows = buf.shape[1]
    ins = [pltpu.make_async_copy(o_ref.at[i * rows:(i + 1) * rows, :], buf.at[i], in_sem.at[i]) for i in range(parts)]
    outs = [pltpu.make_async_copy(buf.at[i], out_ref.at[i * rows:(i + 1) * rows, :], out_sem.at[i]) for i in range(parts)]
    for c in ins:
        c.start()
    sal_ref[...] = s_ref[...]
    for i in range(parts):
        ins[i].wait()
        outs[i].start()
    for c in outs:
        c.wait()


def settle(out, sal, parts=8):
    anyspace, vm = pl.BlockSpec(memory_space=pl.ANY), pl.BlockSpec(memory_space=pltpu.VMEM)
    return pl.pallas_call(
        settle_kernel,
        out_shape=(jax.ShapeDtypeStruct(out.shape, out.dtype), jax.ShapeDtypeStruct(sal.shape, sal.dtype)),
        in_specs=[anyspace, vm],
        out_specs=(anyspace, vm),
        scratch_shapes=[pltpu.VMEM((parts, out.shape[0] // parts, out.shape[1]), out.dtype),
                        pltpu.SemaphoreType.DMA((parts,)), pltpu.SemaphoreType.DMA((parts,))],
        name="settle",
    )(out, sal)


def solution(mesh):
    n_row, n_col = mesh.shape["row"], mesh.shape["col"]

    def body(weight, inverse_rows, pruned_index):
        out, sal = settle(*step(pruned_index[None, :], weight, inverse_rows, n_row, n_col))
        return out, sal[0]

    return jax.shard_map(
        body,
        mesh=mesh,
        in_specs=(P("row", "col"), P("row", "col"), P()),
        out_specs=(P("row", "col"), P("row")),
        check_vma=False,
    )
```
